256 devices in a mesh: ctx: 64 (over z, y, core), hg: 4 (over x).
Axes of the slice: x: 4, y: 4, z: 8, core: 2. Of those that a mesh axis runs over, the one named last changes fastest.
Arguments:
- doc_ids: int32 [32768], P('ctx'), may hold values from 0 to 63, never falling along the last dimension, each value on 1 to 1024 neighbouring positions
- rotated_queries: bfloat16 [32768, 2048], P('ctx', 'hg'), may hold values from -6 to 6
- rotated_keys: bfloat16 [32768, 512], P('ctx', 'hg'), may hold values from -6 to 6
- value_matrix: bfloat16 [32768, 512], P('ctx', 'hg'), may hold values from -6 to 6
- out_proj: bfloat16 [4096, 2048], P('ctx', 'hg'), may hold values from -0.125 to 0.125
- cotangent: bfloat16 [32768, 4096], P('ctx'), may hold values from -16 to 16
Outputs:
- layer_output: bfloat16 [32768, 4096], P('ctx', 'hg')
- query_grad: bfloat16 [32768, 2048], P('ctx', 'hg')
- key_gradient: bfloat16 [32768, 512], P('ctx', 'hg')
- value_gradient: bfloat16 [32768, 512], P('ctx', 'hg')
- proj_grad: bfloat16 [4096, 2048], P('ctx', 'hg')
The draws below stay inside these ranges and needn't reach their ends.
Inputs may be any that keep to these rules, and one draw needn't show every extreme that they name: `doc_ids`: document ids in token order, never falling; every document has 1 to 1024 tokens and one has exactly 1024.
All inputs are finite; a program needn't handle non-finite values.
Results may differ from the reference program's by a relative error of at most 0.013.
Values may be sent and summed in bfloat16 or wider, within the bound.
A program may use at most 128 MiB of HBM per device.

```python
import math
import jax
import jax.numpy as jnp
import numpy as np
from jax import lax

D = 4096
QUERY_HEADS = 16
KEY_VALUE_HEADS = 4
HEAD_SIZE = 128
TOK_DEV = 512
CONTEXT_TOKENS = 32768
DOC_MOST = 1024
DOCS = 64


def starting_sample(key, salted, columns):
    folded = jax.random.fold_in(key, salted)
    return jax.random.truncated_normal(folded, -5.0, 5.0, (CONTEXT_TOKENS, columns), jnp.float32)


def draw_rotated_queries(key, part):
    sampled_items = starting_sample(key, 11, QUERY_HEADS * HEAD_SIZE)
    return sampled_items.astype(jnp.bfloat16)


def draw_rotated_keys(key, part):
    sampled_items = starting_sample(key, 13, KEY_VALUE_HEADS * HEAD_SIZE)
    return sampled_items.astype(jnp.bfloat16)


def with_spikes(values, stream_key, source, target, blocks, factor):
    def block_of(position):
        return (jnp.arange(values.shape[position]) // (values.shape[position] // blocks)).reshape((-1,) + (1,) * (values.ndim - 1 - position))

    near = jax.random.permutation(stream_key, blocks)[block_of(target)]
    far = (block_of(target) + blocks // 2) % blocks
    return jnp.where((block_of(source) == near) | (block_of(source) == far), factor * values, values)


def block_levels(key, extent, shards, low, high):
    loudness = 1.0
    for axis_at, shards_of in shards:
        steps = jax.random.uniform(jax.random.fold_in(jax.random.fold_in(key, 6), axis_at), (shards_of,), jnp.float32, low / len(shards), high / len(shards))
        loudness = loudness * jnp.repeat(jnp.exp(steps), extent[axis_at] // shards_of).reshape((-1,) + (1,) * (len(extent) - 1 - axis_at))
    return loudness


def length_profile(number_of, total, limit, slope):
    loads = [(1 << 20) // math.isqrt(rank ** slope) + 1 for rank in range(2, number_of + 1)]
    spare, holding = total - limit - (number_of - 1), [1] * (number_of - 1)
    while spare > 0:
        candidates = [i for i in range(number_of - 1) if holding[i] < limit]
        whole, remaining = sum([loads[i] for i in candidates]), spare
        for i in candidates:
            more = min(limit - holding[i], max(1, remaining * loads[i] // whole), spare)
            holding[i] = holding[i] + more
            spare = spare - more
    return np.array([limit] + holding)


def ragged_sizes(rng, number_of, total, most, slope):
    if number_of == 2:
        one = jax.random.randint(rng, (), max(1, total - most), min(most, total - 1) + 1)
        return jnp.stack([one, total - one])
    sizes = jnp.asarray(length_profile(number_of, total, most, slope), jnp.int32)
    couples = (number_of - 1) // 2
    donor, sink = sizes[1:1 + 2 * couples:2], sizes[2:2 + 2 * couples:2]
    slack = jnp.minimum(donor - 1, most - sink)
    passed = jax.random.randint(jax.random.fold_in(rng, 1), (couples,), 0, 1 << 20) % (slack + 1)
    sizes = sizes.at[1:1 + 2 * couples:2].set(donor - passed).at[2:2 + 2 * couples:2].set(sink + passed)
    return sizes[jax.random.permutation(jax.random.fold_in(rng, 2), number_of)]


def scatter_about(key, shape, spread, most, shards=(), kind=jnp.bfloat16):
    result = spread * jax.random.normal(key, shape, jnp.float32)
    if shards:
        result = result * block_levels(key, shape, shards, -0.22, 0.18)
    return jnp.clip(result, -most, most).astype(kind)


def bell_draw_with(rng, dims, width, most, split, heavy, kind=jnp.bfloat16):
    array = width * jax.random.normal(rng, dims, jnp.float32)
    if split:
        array = array * block_levels(rng, dims, split, -0.22, 0.18)
    return jnp.clip(with_spikes(array, jax.random.fold_in(rng, 3), *heavy), -most, most).astype(kind)


def setup_inputs(seed: int = 0) -> dict:
    splits = jax.random.split(jax.random.key(seed), 7)
    return {
        "doc_ids": jnp.searchsorted(jnp.cumsum(ragged_sizes(splits[0], DOCS, CONTEXT_TOKENS, DOC_MOST, 1)), jnp.arange(CONTEXT_TOKENS), side="right").astype(jnp.int32),
        "rotated_queries": draw_rotated_queries(jax.random.fold_in(splits[6], 71), 0),
        "rotated_keys": draw_rotated_keys(jax.random.fold_in(splits[6], 71), 0),
        "value_matrix": scatter_about(splits[3], (CONTEXT_TOKENS, KEY_VALUE_HEADS * HEAD_SIZE), 1.0, 6.0, ((0, 64), (1, 4))),
        "out_proj": scatter_about(splits[4], (D, QUERY_HEADS * HEAD_SIZE), (QUERY_HEADS * HEAD_SIZE) ** -0.5, 0.125, ((0, 64), (1, 4))),
        "cotangent": bell_draw_with(splits[5], (CONTEXT_TOKENS, D), 1.0, 16.0, ((0, 64),), (0, 1, 64, 4.0)),
    }


def reference(doc_ids, rotated_queries, rotated_keys, value_matrix, out_proj, cotangent):
    group_length = QUERY_HEADS // KEY_VALUE_HEADS
    score_scale = HEAD_SIZE ** -0.5
    block_rows = TOK_DEV
    block_count = CONTEXT_TOKENS // TOK_DEV
    border_amount = DOC_MOST
    window = DOC_MOST + TOK_DEV
    attention_gradient = jnp.dot(cotangent, out_proj, preferred_element_type=jnp.float32).astype(jnp.bfloat16)
    gradient_heads = attention_gradient.reshape(CONTEXT_TOKENS, KEY_VALUE_HEADS, group_length, HEAD_SIZE)
    query_head_list = rotated_queries.reshape(CONTEXT_TOKENS, KEY_VALUE_HEADS, group_length, HEAD_SIZE)
    padded_keys = jnp.concatenate([jnp.zeros((border_amount, KEY_VALUE_HEADS * HEAD_SIZE), jnp.bfloat16), rotated_keys], 0).reshape(CONTEXT_TOKENS + border_amount, KEY_VALUE_HEADS, HEAD_SIZE)
    padded_values = jnp.concatenate([jnp.zeros((border_amount, KEY_VALUE_HEADS * HEAD_SIZE), jnp.bfloat16), value_matrix], 0).reshape(CONTEXT_TOKENS + border_amount, KEY_VALUE_HEADS, HEAD_SIZE)
    pad_docs = jnp.concatenate([jnp.full((border_amount,), -1, jnp.int32), doc_ids.astype(jnp.int32)], 0)

    def one_block(carried, block_index):
        key_running_total, value_running_total = carried
        start_row = (block_index * block_rows).astype(jnp.int32)
        query_block = lax.dynamic_slice_in_dim(query_head_list, start_row, block_rows, 0).astype(jnp.float32)
        grad_block = lax.dynamic_slice_in_dim(gradient_heads, start_row, block_rows, 0).astype(jnp.float32)
        key_block = lax.dynamic_slice_in_dim(padded_keys, start_row, window, 0).astype(jnp.float32)
        value_block = lax.dynamic_slice_in_dim(padded_values, start_row, window, 0).astype(jnp.float32)
        query_docs = lax.dynamic_slice_in_dim(doc_ids.astype(jnp.int32), start_row, block_rows, 0)
        key_docs = lax.dynamic_slice_in_dim(pad_docs, start_row, window, 0)
        query_pos = start_row + jnp.arange(block_rows, dtype=jnp.int32)
        key_pos = start_row - border_amount + jnp.arange(window, dtype=jnp.int32)
        allowed = (query_docs[:, None] == key_docs[None, :]) & (key_pos[None, :] <= query_pos[:, None])
        scores = jnp.einsum("bkgd,wkd->kgbw", query_block, key_block) * score_scale
        masked = jnp.where(allowed, scores, -jnp.inf)
        row_max = jnp.max(masked, axis=3, keepdims=True)
        row_sum = jnp.sum(jnp.where(allowed, jnp.exp(masked - row_max), 0.0), axis=3, keepdims=True)
        log_total = row_max + jnp.log(row_sum)
        weights = jnp.where(allowed, jnp.exp(masked - log_total), 0.0)
        weights = lax.optimization_barrier(weights.astype(jnp.bfloat16)).astype(jnp.float32)
        attended = jnp.einsum("kgbw,wkd->bkgd", weights, value_block).astype(jnp.bfloat16)
        attended_wide = lax.optimization_barrier(attended).astype(jnp.float32)
        row_delta = jnp.einsum("bkgd,bkgd->kgb", grad_block, attended_wide)[..., None]
        grad_dots = jnp.einsum("bkgd,wkd->kgbw", grad_block, value_block)
        shifted = (weights * (grad_dots - row_delta) * score_scale).astype(jnp.bfloat16)
        shifted = lax.optimization_barrier(shifted).astype(jnp.float32)
        query_grad = jnp.einsum("kgbw,wkd->bkgd", shifted, key_block).astype(jnp.bfloat16)
        key_part = jnp.einsum("kgbw,bkgd->wkd", shifted, query_block)
        value_part = jnp.einsum("kgbw,bkgd->wkd", weights, grad_block)
        key_running_total = lax.dynamic_update_slice_in_dim(key_running_total, lax.dynamic_slice_in_dim(key_running_total, start_row, window, 0) + key_part, start_row, 0)
        value_running_total = lax.dynamic_update_slice_in_dim(value_running_total, lax.dynamic_slice_in_dim(value_running_total, start_row, window, 0) + value_part, start_row, 0)
        return (key_running_total, value_running_total), (attended, query_grad)

    zeroed_running_total = jnp.zeros((CONTEXT_TOKENS + border_amount, KEY_VALUE_HEADS, HEAD_SIZE), jnp.float32)
    (key_running_total, value_running_total), (attended, query_grad) = lax.scan(one_block, (zeroed_running_total, zeroed_running_total), jnp.arange(block_count, dtype=jnp.int32))
    attended = attended.reshape(CONTEXT_TOKENS, QUERY_HEADS * HEAD_SIZE)
    layer_output = jnp.dot(attended, out_proj.T, preferred_element_type=jnp.float32).astype(jnp.bfloat16)
    proj_grad = jnp.dot(cotangent.T, attended, preferred_element_type=jnp.float32).astype(jnp.bfloat16)
    query_grad = query_grad.reshape(CONTEXT_TOKENS, QUERY_HEADS * HEAD_SIZE)
    key_gradient = key_running_total[border_amount:].reshape(CONTEXT_TOKENS, KEY_VALUE_HEADS * HEAD_SIZE).astype(jnp.bfloat16)
    value_gradient = value_running_total[border_amount:].reshape(CONTEXT_TOKENS, KEY_VALUE_HEADS * HEAD_SIZE).astype(jnp.bfloat16)
    return (layer_output, query_grad, key_gradient, value_gradient, proj_grad)
```

```python
import jax
import jax.numpy as jnp
from jax import lax
from jax.experimental import pallas as pl
from jax.experimental.pallas import tpu as pltpu
from jax.sharding import PartitionSpec as P

MESH = pl.DeviceIdType.MESH
BF = jnp.bfloat16
F32 = jnp.float32
I32 = jnp.int32
DMA = pltpu.SemaphoreType.DMA

HEAD = 128
HEADS = 4
TOK = 512
QB = 256
KW = 1280
WIN = 1536
NX, NY, NZ = 4, 4, 8
CTX = 64
SCALE = HEAD ** (-0.5)
EXP_SCALE = SCALE * 1.4426950408889634
MASKED = -1e30


def nn(a, b):
    return jnp.dot(a, b, preferred_element_type=F32)


def nt(a, b):
    return lax.dot_general(a, b, (((1,), (1,)), ((), ())), preferred_element_type=F32)


def al(value, by):
    return pl.multiple_of(value, by)


def kernel(
    doc_ref, q_ref, k_ref, v_ref, w_ref, cot_hbm,
    out_ref, qg_ref, kg_ref, vg_ref, pg_ref,
    cot, kwin, vwin, dwin, kt, vt, wall, st_ref, pbuf, dsbuf, att_t, att, inv_l, d_o, dos, qs, dk, dv,
    gbuf, drecv, gh, yr1, yr2, yh, zr, fts, frec, lbuf, xr1, xr2, gks, gkr,
    cot_sem, hs, hr, zs_w, zr_w, ys_w, yr_w, rs_w, rr_w, ps_w, pr_w,
    ds_s, dr_s, y1s, y1r, y2s, y2r, zs_g, zr_g, fs, fr, x1s, x1r, x2s, x2r, gs, gr,
):
    c = lax.axis_index("ctx")
    x = lax.axis_index("hg")
    z = lax.div(c, 8)
    y = lax.rem(lax.div(c, 2), NY)
    k = lax.rem(c, 2)

    def at_ctx(by):
        return (lax.rem(c + by + CTX, CTX), x)

    def at_z(by):
        return (lax.rem(z + by, NZ) * 8 + y * 2 + k, x)

    def at_y(by):
        return (z * 8 + lax.rem(y + by, NY) * 2 + k, x)

    def at_x(by):
        return (c, lax.rem(x + by, NX))

    partner = (z * 8 + y * 2 + (1 - k), x)

    def rcopy(src, dst, send, recv, device):
        return pltpu.make_async_remote_copy(
            src_ref=src, dst_ref=dst, send_sem=send, recv_sem=recv,
            device_id=device, device_id_type=MESH,
        )

    cot_copy = pltpu.make_async_copy(cot_hbm, cot, cot_sem)
    cot_copy.start()

    barrier = pltpu.get_barrier_semaphore()
    peers = [partner, at_y(1), at_y(3), at_x(1), at_x(3), at_ctx(1), at_ctx(2), at_ctx(-1), at_ctx(-2)]
    peers += [at_z(d) for d in range(1, NZ)]
    for peer in peers:
        pl.semaphore_signal(barrier, inc=1, device_id=peer, device_id_type=MESH)
    pl.semaphore_wait(barrier, len(peers))

    own_parts = ((doc_ref, dwin, 0), (k_ref, kwin, 1), (v_ref, vwin, 2))

    def piece(ref, index, at):
        return ref.at[at] if index == 0 else ref.at[pl.ds(at * TOK, TOK)]

    def halo_next(i):
        mine, ref, n = own_parts[i]
        return rcopy(mine, piece(ref, n, 1), hs.at[0, n], hr.at[1, n], at_ctx(1))

    def halo_far(i):
        mine, ref, n = own_parts[i]
        return rcopy(mine, piece(ref, n, 0), hs.at[1, n], hr.at[0, n], at_ctx(2))

    def halo_relay(i):
        _, ref, n = own_parts[i]
        return rcopy(piece(ref, n, 1), piece(ref, n, 0), hs.at[2, n], hr.at[0, n], partner)

    for i in range(3):
        halo_next(i).start()

        @pl.when(k == 0)
        def _():
            halo_far(i).start()

    def half_rows(a):
        return pl.ds(32 * a, 32)

    def gather_z(a, d):
        return rcopy(
            w_ref.at[half_rows(a)], wall.at[z, y, k, half_rows(a)], zs_w.at[a, d], zr_w.at[a, d], at_z(d)
        )

    def slab(yy, a):
        return wall.at[:, yy, k, half_rows(a)]

    def gather_y(a, side):
        return rcopy(slab(y, a), slab(y, a), ys_w.at[a, side], yr_w.at[a, side], at_y(1 if side == 0 else 3))

    def gather_relay(a, side):
        src = wall.at[pl.ds(4 * side, 4), lax.rem(y + (3 if side == 0 else 1), NY), k, half_rows(a)]
        return rcopy(src, src, rs_w.at[a, side], rr_w.at[a, side], at_y(1 if side == 0 else 3))

    def gather_partner(a, which):
        src = slab(lax.rem(y + (0, 3, 1, 2)[which], NY), a)
        return rcopy(src, src, ps_w.at[a, which], pr_w.at[a, which], partner)

    far_first = (4, 3, 5, 2, 6, 1, 7)
    for a in range(2):
        for d in far_first:
            gather_z(a, d).start()

    wall[z, y, k] = w_ref[...]
    kwin[pl.ds(2 * TOK, TOK)] = k_ref[...]
    vwin[pl.ds(2 * TOK, TOK)] = v_ref[...]
    dwin[2] = doc_ref[...]
    dk[...] = jnp.zeros_like(dk)
    dv[...] = jnp.zeros_like(dv)

    for i in range(3):
        halo_next(i).wait_recv()

        @pl.when(k == 0)
        def _():
            halo_relay(i).start()

    for i in range(3):
        halo_far(i).wait_recv()

    def gather_after_z(a):
        for d in range(1, NZ):
            gather_z(a, d).wait_recv()
        gather_y(a, 0).start()
        gather_y(a, 1).start()
        gather_partner(a, 0).start()

    def gather_after_y(a):
        for side in range(2):
            gather_y(a, side).wait_recv()
            gather_relay(a, side).start()
            gather_partner(a, 1 + side).start()

    def gather_after_relay(a):
        for side in range(2):
            gather_relay(a, side).wait_recv()
        gather_partner(a, 3).start()

    gather_after_z(0)

    doc_row = dwin[2].astype(F32)
    start = jnp.zeros((1, TOK), F32)
    for p in range(3):
        column = jnp.broadcast_to(dwin[p].astype(F32), (128, TOK)).T
        counts = [
            jnp.sum(jnp.where(column < doc_row[:, 128 * b : 128 * b + 128], 1.0, 0.0), axis=0, keepdims=True)
            for b in range(TOK // 128)
        ]
        count = jnp.concatenate(counts, 1)
        start = start + (jnp.where(c >= 2 - p, count, float(TOK)) if p < 2 else count)
    start = start.astype(I32)
    for b in range(2):
        st_ref[b] = start[:, QB * b : QB * b + QB] - QB * b

    k_turned = kwin[...].astype(F32).T.astype(BF)
    v_turned = vwin[...].astype(F32).T.astype(BF)
    for b in range(2):
        kt[b] = k_turned[:, QB * b : QB * b + KW]
        vt[b] = v_turned[:, QB * b : QB * b + KW]

    @pl.loop(0, 2 * HEADS)
    def _(t):
        b = lax.div(t, HEADS)
        h = lax.rem(t, HEADS)
        rows = pl.ds(al(b * QB, QB), QB)
        heads = pl.ds(al(h * HEAD, HEAD), HEAD)
        lanes = pl.ds(al(h * QB, QB), QB)
        scores = nt(kwin[pl.ds(al(b * QB, QB), KW), :], q_ref[rows, heads])
        key_at = lax.broadcasted_iota(I32, (KW, QB), 0)
        last = lax.broadcasted_iota(I32, (1, QB), 1) + 2 * TOK
        scores = jnp.where((key_at >= st_ref[b]) & (key_at <= last), scores, MASKED)
        top = jnp.max(scores, axis=0, keepdims=True)
        weights = jnp.exp2(scores * EXP_SCALE - top * EXP_SCALE)
        total = 1.0 / jnp.sum(weights, axis=0, keepdims=True)
        weights = weights.astype(BF)
        pbuf[b, :, lanes] = weights
        inv_l[t] = total
        turned = nn(vt[b], weights) * total
        att_t[heads, rows] = turned.astype(BF)
        att[rows, heads] = turned.T.astype(BF)

        @pl.when(t == 1)
        def _():
            gather_after_z(1)

        @pl.when(t == 3)
        def _():
            gather_after_y(0)

        @pl.when(t == 6)
        def _():
            gather_after_y(1)

    cot_copy.wait()

    @pl.loop(0, NZ)
    def _(zz):
        term = nn(att_t[...], cot[:, pl.ds(al(zz * TOK, TOK), TOK)]).astype(BF)
        for yy in range(NY):
            gbuf[zz, yy] = term[:, 128 * yy : 128 * yy + 128]

    def pair_send(q):
        return rcopy(
            gbuf.at[:, :, pl.ds(al((1 - k) * 256 + 128 * q, 128), 128), :],
            drecv.at[q], ds_s.at[q], dr_s.at[q], partner,
        )

    for q in range(2):
        pair_send(q).start()

    for a in range(2):
        gather_after_relay(a)
    for a in range(2):
        for which in range(4):
            gather_partner(a, which).wait_recv()

    def layer_term(r):
        owner = lax.rem(x + r, NX)

        @pl.loop(0, 2)
        def _(e):
            rows = wall[owner * 2 + e].reshape(TOK, TOK)
            lbuf[r, e] = nt(att[...], rows).astype(BF)

    def x_first(side):
        return rcopy(lbuf.at[2, side], xr1.at[side], x1s.at[side], x1r.at[side], at_x(1 if side == 0 else 3))

    def x_second(side, e):
        return rcopy(
            lbuf.at[1 if side == 0 else 3, e], xr2.at[side, e], x2s.at[side, e], x2r.at[side, e],
            at_x(1 if side == 0 else 3),
        )

    layer_term(2)
    x_first(0).start()
    x_first(1).start()
    layer_term(1)
    x_second(0, 1).start()
    layer_term(3)
    x_second(1, 0).start()
    layer_term(0)

    def y_first(q, side):
        return rcopy(
            gh.at[q, lax.rem(y + 2, NY), pl.ds(4 * side, 4)], yr1.at[q, side],
            y1s.at[q, side], y1r.at[q, side], at_y(1 if side == 0 else 3),
        )

    def y_second(q, side, e):
        return rcopy(
            gh.at[q, lax.rem(y + (1 if side == 0 else 3), NY), pl.ds(4 * e, 4)], yr2.at[q, side, e],
            y2s.at[q, side, e], y2r.at[q, side, e], at_y(1 if side == 0 else 3),
        )

    def grad_pair(q):
        pair_send(q).wait_recv()
        rows = pl.ds(al(k * 256 + 128 * q, 128), 128)

        @pl.loop(0, NZ)
        def _(zz):
            for yy in range(NY):
                gh[q, yy, zz] = (gbuf[zz, yy, rows, :].astype(F32) + drecv[q, zz, yy].astype(F32)).astype(BF)

        y_first(q, 0).start()
        y_first(q, 1).start()
        y_second(q, 0, 1).start()
        y_second(q, 1, 0).start()

    def grad_y_first(q):
        for side in range(2):
            y_first(q, side).wait_recv()
            owner = lax.rem(y + (1 if side == 0 else 3), NY)
            here = pl.ds(4 * side, 4)
            gh[q, owner, here] = (gh[q, owner, here].astype(F32) + yr1[q, side].astype(F32)).astype(BF)
            y_second(q, side, side).start()

    def grad_z(q, d):
        return rcopy(yh.at[q, lax.rem(z + d, NZ)], zr.at[q, d - 1], zs_g.at[q, d], zr_g.at[q, d], at_z(d))

    def grad_y_last(q):
        for side in range(2):
            for e in range(2):
                y_second(q, side, e).wait_recv()
        for e in range(2):
            here = pl.ds(4 * e, 4)
            total = gh[q, y, here].astype(F32) + yr2[q, 0, e].astype(F32) + yr2[q, 1, e].astype(F32)
            yh[q, here] = total.astype(BF)
        for d in far_first:
            grad_z(q, d).start()

    for q in range(2):
        grad_pair(q)

    @pl.loop(0, 2)
    def _(n):
        lanes = pl.ds(al(n * 256, 256), 256)
        d_o[:, lanes] = nn(cot[...], wall[:, :, :, :, lanes].reshape(4096, 256)).astype(BF)

    def x_add(side):
        x_first(side).wait_recv()
        r = 1 if side == 0 else 3
        lbuf[r, side] = (lbuf[r, side].astype(F32) + xr1[side].astype(F32)).astype(BF)
        x_second(side, side).start()

    @pl.loop(0, 2)
    def _(b):
        rows = pl.ds(al(b * QB, QB), QB)
        keys = pl.ds(al(b * QB, QB), KW)

        @pl.loop(0, HEADS)
        def _(h):
            heads = pl.ds(al(h * HEAD, HEAD), HEAD)
            lanes = pl.ds(al(h * QB, QB), QB)
            total = inv_l[b * HEADS + h]
            grad = d_o[rows, heads]
            turned = grad.astype(F32).T
            delta = jnp.sum(turned * att_t[heads, rows].astype(F32), axis=0, keepdims=True)
            dots = nt(vwin[keys, :], grad)
            shifted = (pbuf[b, :, lanes].astype(F32) * ((dots - delta) * (total * SCALE))).astype(BF)
            dsbuf[:, lanes] = shifted
            qg_ref[rows, heads] = nn(kt[b], shifted).T.astype(BF)
            dos[lanes, :] = (turned * total).T.astype(BF)
            qs[lanes, :] = q_ref[rows, heads]

            t = b * HEADS + h

            @pl.when(t == 1)
            def _():
                x_add(0)
                x_add(1)
                grad_y_first(0)

            @pl.when(t == 3)
            def _():
                grad_y_first(1)

            @pl.when(t == 5)
            def _():
                grad_y_last(0)

        dk[keys, :] += nn(dsbuf[...], qs[...])
        dv[keys, :] += nn(pbuf[b], dos[...])

    def grad_back(s):
        return rcopy(gks.at[s], gkr.at[s], gs.at[s], gr.at[s], at_ctx(s - 2))

    for s in range(2):
        gks[s, 0] = dk[pl.ds(s * TOK, TOK)].astype(BF)
        gks[s, 1] = dv[pl.ds(s * TOK, TOK)].astype(BF)
        grad_back(s).start()

    grad_y_last(1)

    sums = []
    for q in range(2):
        total = yh[q, z].astype(F32)
        for d in range(1, NZ):
            grad_z(q, d).wait_recv()
            total = total + zr[q, d - 1].astype(F32)
        sums.append(total.T)
    turned = jnp.concatenate(sums, 1).astype(BF)
    fts[0] = turned[0:64]
    fts[1] = turned[64:128]

    final = rcopy(fts.at[1 - k], frec, fs, fr, partner)
    final.start()

    for s in range(2):
        grad_back(s).wait_recv()
    for n, (acc, ref) in enumerate(((dk, kg_ref), (dv, vg_ref))):
        total = acc[pl.ds(2 * TOK, TOK)] + gkr[0, n].astype(F32) + gkr[1, n].astype(F32)
        ref[...] = total.astype(BF)

    final.wait_recv()
    mine, other = fts[k], frec[...]
    pg_ref[:, 0:256] = jnp.where(k == 0, mine, other)
    pg_ref[:, 256:512] = jnp.where(k == 0, other, mine)

    for e in range(2):
        for side in range(2):
            x_second(side, e).wait_recv()
        total = lbuf[0, e].astype(F32) + xr2[0, e].astype(F32) + xr2[1, e].astype(F32)
        out_ref[:, 512 * e : 512 * e + 512] = total.astype(BF)

    for i in range(3):
        halo_next(i).wait_send()

        @pl.when(k == 0)
        def _():
            halo_far(i).wait_send()
            halo_relay(i).wait_send()

    for a in range(2):
        for d in range(1, NZ):
            gather_z(a, d).wait_send()
        for side in range(2):
            gather_y(a, side).wait_send()
            gather_relay(a, side).wait_send()
        for which in range(4):
            gather_partner(a, which).wait_send()
    for q in range(2):
        pair_send(q).wait_send()
        for side in range(2):
            y_first(q, side).wait_send()
            for e in range(2):
                y_second(q, side, e).wait_send()
        for d in range(1, NZ):
            grad_z(q, d).wait_send()
    final.wait_send()
    for side in range(2):
        x_first(side).wait_send()
        for e in range(2):
            x_second(side, e).wait_send()
    for s in range(2):
        grad_back(s).wait_send()


def body(doc_ids, rotated_queries, rotated_keys, value_matrix, out_proj, cotangent):
    vmem = pl.BlockSpec(memory_space=pltpu.VMEM)
    shape = jax.ShapeDtypeStruct

    def buf(*dims, kind=BF):
        return pltpu.VMEM(dims, kind)

    return tuple(
        pl.pallas_call(
            kernel,
            out_shape=(
                shape((TOK, 1024), BF), shape((TOK, TOK), BF), shape((TOK, HEAD), BF),
                shape((TOK, HEAD), BF), shape((64, TOK), BF),
            ),
            in_specs=[vmem] * 5 + [pl.BlockSpec(memory_space=pl.ANY)],
            out_specs=(vmem,) * 5,
            scratch_shapes=[
                buf(TOK, 4096), buf(WIN, HEAD), buf(WIN, HEAD), buf(3, 1, TOK, kind=I32),
                buf(2, HEAD, KW), buf(2, HEAD, KW), buf(NZ, NY, 2, 64, TOK), buf(2, 1, QB, kind=I32),
                buf(2, KW, HEADS * QB), buf(KW, HEADS * QB), buf(TOK, TOK), buf(TOK, TOK),
                buf(2 * HEADS, 1, QB, kind=F32), buf(TOK, TOK), buf(HEADS * QB, HEAD), buf(HEADS * QB, HEAD),
                buf(WIN, HEAD, kind=F32), buf(WIN, HEAD, kind=F32),
                buf(NZ, NY, TOK, 128), buf(2, NZ, NY, 128, 128), buf(2, NY, NZ, 128, 128),
                buf(2, 2, 4, 128, 128), buf(2, 2, 2, 4, 128, 128), buf(2, NZ, 128, 128),
                buf(2, NZ - 1, 128, 128), buf(2, 64, 256), buf(64, 256),
                buf(NX, 2, TOK, TOK), buf(2, TOK, TOK), buf(2, 2, TOK, TOK),
                buf(2, 2, TOK, HEAD), buf(2, 2, TOK, HEAD),
                DMA, DMA((3, 3)), DMA((2, 3)), DMA((2, NZ)), DMA((2, NZ)), DMA((2, 2)), DMA((2, 2)),
                DMA((2, 2)), DMA((2, 2)), DMA((2, 4)), DMA((2, 4)),
                DMA((2,)), DMA((2,)), DMA((2, 2)), DMA((2, 2)), DMA((2, 2, 2)), DMA((2, 2, 2)),
                DMA((2, NZ)), DMA((2, NZ)), DMA, DMA, DMA((2,)), DMA((2,)), DMA((2, 2)), DMA((2, 2)),
                DMA((2,)), DMA((2,)),
            ],
            compiler_params=pltpu.CompilerParams(
                collective_id=0, has_side_effects=True, vmem_limit_bytes=64 * 1024 * 1024 - 65536
            ),
        )(doc_ids.reshape(1, TOK), rotated_queries, rotated_keys, value_matrix, out_proj, cotangent)
    )


def solution(mesh):
    in_specs = (P("ctx"), P("ctx", "hg"), P("ctx", "hg"), P("ctx", "hg"), P("ctx", "hg"), P("ctx", None))
    out_specs = (P("ctx", "hg"),) * 5
    return jax.shard_map(body, mesh=mesh, in_specs=in_specs, out_specs=out_specs, check_vma=False)
```

```python
import jax
import jax.numpy as jnp
from jax import lax
from jax.experimental import pallas as pl
from jax.experimental.pallas import tpu as pltpu
from jax.sharding import PartitionSpec as P

MESH = pl.DeviceIdType.MESH
BF = jnp.bfloat16
F32 = jnp.float32
I32 = jnp.int32
DMA = pltpu.SemaphoreType.DMA

HEAD = 128
HEADS = 4
TOK = 512
QB = 256
KW = 1280
WIN = 1536
NX, NY, NZ = 4, 4, 8
CTX = 64
SCALE = HEAD ** (-0.5)
EXP_SCALE = SCALE * 1.4426950408889634
MASKED = -1e30
VMEM_LIMIT = 64 * 1024 * 1024 - 65536
UNITS = (
    (0, (0, 0)), (1, (0, 0)), (0, (3, 1)), (1, (3, 1)), (0, (1, 3)), (1, (1, 3)), (0, (2, 2)), (1, (2, 2)),
)
CHUNKS = ((0, 112), (112, 112), (224, 32))


def nn(a, b):
    return jnp.dot(a, b, preferred_element_type=F32)


def nt(a, b):
    return lax.dot_general(a, b, (((1,), (1,)), ((), ())), preferred_element_type=F32)


def al(value, by):
    return pl.multiple_of(value, by)


def kernel(
    doc_hbm, q_hbm, k_hbm, v_hbm, w_hbm, cot_hbm,
    out_hbm, qg_hbm, kg_hbm, vg_hbm, pg_hbm,
    doc_ref, q_ref, k_ref, v_ref, w_ref, out_ref, qg_ref, kg_ref, vg_ref, pg_ref,
    cot, kwin, vwin, dwin, kt, vt, wall, st_ref, pbuf, dsbuf, att_t, att, inv_l, delta, d_o, dos, qs, dk, dv,
    gbuf, drecv, gh, yr1, yr2, yh, zr, gz, zre, gy, yrl, fts, frec, lbuf, xr1, xr2, gks, gkr,
    vrel, vs, vr, cot_sem, in_sem, out_sem, hs, hr, az_s, az_r, ao_s, ao_r, ys_w, yr_w, rs_w, rr_w, ps_w, pr_w,
    ds_s, dr_s, y1s, y1r, y2s, y2r, zs_g, zr_g, zs_e, zr_e, ys_l, yr_l, fs, fr, x1s, x1r, x2s, x2r, gs, gr,
):
    c = lax.axis_index("ctx")
    x = lax.axis_index("hg")
    z = lax.div(c, 8)
    y = lax.rem(lax.div(c, 2), NY)
    k = lax.rem(c, 2)

    def at_ctx(by):
        return (lax.rem(c + by + CTX, CTX), x)

    def at_z(by):
        return (lax.rem(z + by, NZ) * 8 + y * 2 + k, x)

    def at_y(by):
        return (z * 8 + lax.rem(y + by, NY) * 2 + k, x)

    def at_x(by):
        return (c, lax.rem(x + by, NX))

    partner = (z * 8 + y * 2 + (1 - k), x)

    def rcopy(src, dst, send, recv, device):
        return pltpu.make_async_remote_copy(
            src_ref=src, dst_ref=dst, send_sem=send, recv_sem=recv,
            device_id=device, device_id_type=MESH,
        )

    barrier = pltpu.get_barrier_semaphore()
    peers = [partner, at_y(1), at_y(3), at_x(1), at_x(3), at_ctx(1), at_ctx(2), at_ctx(-1), at_ctx(-2)]
    peers += [at_z(d) for d in range(1, NZ)]
    for peer in peers:
        pl.semaphore_signal(barrier, inc=1, device_id=peer, device_id_type=MESH)
    ins = ((w_hbm, w_ref), (k_hbm, k_ref), (doc_hbm, doc_ref), (v_hbm, v_ref), (q_hbm, q_ref))
    ins = [pltpu.make_async_copy(src, dst, in_sem.at[i]) for i, (src, dst) in enumerate(ins)]
    outs = ((out_ref, out_hbm), (qg_ref, qg_hbm), (kg_ref, kg_hbm), (vg_ref, vg_hbm), (pg_ref, pg_hbm))
    outs = [pltpu.make_async_copy(src, dst, out_sem.at[i]) for i, (src, dst) in enumerate(outs)]
    cot_copy = pltpu.make_async_copy(cot_hbm, cot, cot_sem)
    for copy in ins:
        copy.start()
    cot_copy.start()
    for copy in ins:
        copy.wait()
    pl.semaphore_wait(barrier, len(peers))

    own_parts = ((doc_ref, dwin, 0), (k_ref, kwin, 1), (v_ref, vwin, 2))

    def piece(ref, index, at):
        return ref.at[at] if index == 0 else ref.at[pl.ds(at * TOK, TOK)]

    def halo_next(i):
        mine, ref, n = own_parts[i]
        return rcopy(mine, piece(ref, n, 1), hs.at[0, n], hr.at[1, n], at_ctx(1))

    def halo_far(i):
        mine, ref, n = own_parts[i]
        return rcopy(mine, piece(ref, n, 0), hs.at[1, n], hr.at[0, n], at_ctx(2))

    def halo_relay(i):
        _, ref, n = own_parts[i]
        return rcopy(piece(ref, n, 1), piece(ref, n, 0), hs.at[2, n], hr.at[0, n], partner)

    def shard(zz):
        return wall.at[zz, y, k]

    def gather_z(way, d):
        to = at_z(d if way == 0 else NZ - d)
        return rcopy(w_ref, shard(z), az_s.at[way, d - 1], az_r.at[way, d - 1], to)

    def gather_on(way, d):
        zz = lax.rem(z + (NZ - 2 if way == 0 else 2), NZ)
        rows = pl.ds(0, 64) if d == 1 else pl.ds(32 * way, 32)
        src = wall.at[zz, y, k, rows]
        return rcopy(src, src, ao_s.at[way, d - 1], ao_r.at[way, d - 1], at_z(d if way == 0 else NZ - d))

    def slab(back, part):
        return wall.at[pl.ds(4 * part, 4), lax.rem(y + back, NY), k]

    def gather_y(side, part):
        return rcopy(slab(0, part), slab(0, part), ys_w.at[side, part], yr_w.at[side, part], at_y(1 if side == 0 else 3))

    def gather_relay(side):
        src = slab(3 if side == 0 else 1, side)
        return rcopy(src, src, rs_w.at[side], rr_w.at[side], at_y(1 if side == 0 else 3))

    def pass_on(back, part):
        return rcopy(slab(back, part), slab(back, part), ps_w.at[back, part], pr_w.at[back, part], partner)

    def gather_first_parts():
        for side in range(2):
            gather_y(side, side).wait_recv()
            gather_relay(side).start()
            pass_on(3 if side == 0 else 1, side).start()

    def gather_second_parts():
        for side in range(2):
            gather_y(side, 1 - side).wait_recv()
            pass_on(3 if side == 0 else 1, 1 - side).start()

    def gather_far_parts():
        for side in range(2):
            gather_relay(side).wait_recv()
            pass_on(2, side).start()

    def slabs_ready(backs):
        for part in range(2):
            pass_on(backs[part], part).wait_recv()

    def halo_starts(i):
        halo_next(i).start()

        @pl.when(k == 0)
        def _():
            halo_far(i).start()

    last_y = y == NY - 1
    first_y = y == 0
    values_up = rcopy(v_ref, vrel, vs.at[0], vr, at_y(1))
    values_on = rcopy(vrel, piece(vwin, 2, 0), vs.at[1], hr.at[0, 2], at_z(1))
    values_swap = rcopy(piece(vwin, 2, 0), piece(vwin, 2, 1), hs.at[2, 2], hr.at[1, 2], partner)

    halo_starts(0)
    halo_starts(1)

    @pl.when(jnp.logical_not(last_y))
    def _():
        halo_starts(2)

    @pl.when(last_y)
    def _():
        values_up.start()

        @pl.when(k == 0)
        def _():
            halo_next(2).start()

    for d in (2, 1):
        for way in range(2):
            gather_z(way, d).start()

    wall[z, y, k] = w_ref[...]
    kwin[pl.ds(2 * TOK, TOK)] = k_ref[...]
    vwin[pl.ds(2 * TOK, TOK)] = v_ref[...]
    dwin[2] = doc_ref[...]
    dk[...] = jnp.zeros_like(dk)
    dv[...] = jnp.zeros_like(dv)

    def gather_middle():
        for way in range(2):
            gather_z(way, 2).wait_recv()
            gather_on(way, 2).start()
            gather_on(way, 1).start()

    def halo_arrives(i):
        halo_next(i).wait_recv()

        @pl.when(k == 0)
        def _():
            halo_relay(i).start()

    def gather_along_y():
        for way in range(2):
            gather_z(way, 1).wait_recv()
            gather_on(way, 1).wait_recv()
        for way in range(2):
            gather_on(way, 2).wait_recv()
        for part in range(2):
            for side in range(2):
                gather_y(side, part if side == 0 else 1 - part).start()
        for part in range(2):
            pass_on(0, part).start()

    halo_arrives(0)
    halo_arrives(1)

    @pl.when(jnp.logical_not(last_y))
    def _():
        gather_middle()

    for i in range(2):
        halo_far(i).wait_recv()

    doc_row = dwin[2].astype(F32)
    start = jnp.zeros((1, TOK), F32)
    for p in range(3):
        column = jnp.broadcast_to(dwin[p].astype(F32), (128, TOK)).T
        counts = [
            jnp.sum(jnp.where(column < doc_row[:, 128 * b : 128 * b + 128], 1.0, 0.0), axis=0, keepdims=True)
            for b in range(TOK // 128)
        ]
        count = jnp.concatenate(counts, 1)
        start = start + (jnp.where(c >= 2 - p, count, float(TOK)) if p < 2 else count)
    start = start.astype(I32)
    for b in range(2):
        st_ref[b] = start[:, QB * b : QB * b + QB] - QB * b

    def x_first(u, side):
        return rcopy(lbuf.at[u, 2, side], xr1.at[u, side], x1s.at[u, side], x1r.at[u, side], at_x(1 if side == 0 else 3))

    def x_second(u, side, e):
        return rcopy(
            lbuf.at[u, 1 if side == 0 else 3, e], xr2.at[u, side, e], x2s.at[u, side, e], x2r.at[u, side, e],
            at_x(1 if side == 0 else 3),
        )

    def layer_unit(u):
        b, backs = UNITS[u]
        for part in range(2):
            rows = wall[pl.ds(4 * part, 4), lax.rem(y + backs[part], NY)].reshape(TOK, TOK)
            term = nt(att[pl.ds(b * QB, QB)], rows).astype(BF)
            for owner in range(2):
                for e in range(2):
                    at = 256 * owner + 128 * e
                    lbuf[u, lax.rem(2 * part + owner - x + NX, NX), e] = term[:, at : at + 128]
        x_first(u, 0).start()
        x_first(u, 1).start()
        x_second(u, 0, 1).start()
        x_second(u, 1, 0).start()

    def layer_second(u):
        for side in range(2):
            x_first(u, side).wait_recv()
            r = 1 if side == 0 else 3
            lbuf[u, r, side] = (lbuf[u, r, side].astype(F32) + xr1[u, side].astype(F32)).astype(BF)
            x_second(u, side, side).start()

    def layer_last(u):
        b, backs = UNITS[u]
        back = jnp.where(x < 2, backs[0], backs[1])
        for e in range(2):
            for side in range(2):
                x_second(u, side, e).wait_recv()
            total = lbuf[u, 0, e].astype(F32) + xr2[u, 0, e].astype(F32) + xr2[u, 1, e].astype(F32)
            lanes = pl.ds(al(512 * e + 128 * lax.rem(y + back, NY), 128), 128)
            out_ref[pl.ds(b * QB, QB), lanes] = total.astype(BF)

    def layer_sent(u):
        for side in range(2):
            x_first(u, side).wait_send()
            for e in range(2):
                x_second(u, side, e).wait_send()

    def attend(t):
        b = lax.div(t, HEADS)
        h = lax.rem(t, HEADS)
        rows = pl.ds(al(b * QB, QB), QB)
        heads = pl.ds(al(h * HEAD, HEAD), HEAD)
        scores = nt(kwin[pl.ds(al(b * QB, QB), KW), :], q_ref[rows, heads])
        key_at = lax.broadcasted_iota(I32, (KW, QB), 0)
        last = lax.broadcasted_iota(I32, (1, QB), 1) + 2 * TOK
        scores = jnp.where((key_at >= st_ref[b]) & (key_at <= last), scores, MASKED)
        top = jnp.max(scores, axis=0, keepdims=True)
        weights = jnp.exp2(scores * EXP_SCALE - top * EXP_SCALE)
        inv_l[t] = 1.0 / jnp.sum(weights, axis=0, keepdims=True)
        pbuf[b, :, pl.ds(al(h * QB, QB), QB)] = weights.astype(BF)

    def gather_values(t):
        b = lax.div(t, HEADS)
        h = lax.rem(t, HEADS)
        rows = pl.ds(al(b * QB, QB), QB)
        heads = pl.ds(al(h * HEAD, HEAD), HEAD)
        turned = nn(vt[b], pbuf[b, :, pl.ds(al(h * QB, QB), QB)]) * inv_l[t]
        att_t[heads, rows] = turned.astype(BF)
        att[rows, heads] = turned.T.astype(BF)

    @pl.loop(0, HEADS)
    def _(t):
        attend(t)

        @pl.when((t == 0) & first_y)
        def _():
            values_up.wait_recv()
            values_on.start()

        @pl.when((t == 1) & last_y)
        def _():
            gather_middle()

        @pl.when((t == 1) & jnp.logical_not(last_y))
        def _():
            gather_along_y()

    @pl.when(first_y)
    def _():
        halo_far(2).wait_recv()

        @pl.when(k == 1)
        def _():
            values_swap.start()

        halo_next(2).wait_recv()

    @pl.when(jnp.logical_not(first_y))
    def _():
        halo_arrives(2)
        halo_far(2).wait_recv()

    v_turned = vwin[...].astype(F32).T.astype(BF)
    for b in range(2):
        vt[b] = v_turned[:, QB * b : QB * b + KW]

    odd = lax.rem(y, 2) == 1
    even = jnp.logical_not(odd)

    @pl.loop(0, HEADS)
    def _(t):
        gather_values(t)

        @pl.when((t == 0) & last_y)
        def _():
            gather_along_y()

    slabs_ready((0, 0))
    layer_unit(0)

    @pl.loop(HEADS, 2 * HEADS)
    def _(t):
        attend(t)
        gather_values(t)

        @pl.when((t == 6) & odd)
        def _():
            gather_first_parts()

    layer_unit(1)

    def pair_send(quarter):
        zs = pl.ds(al(2 * quarter, 2), 2)
        return rcopy(
            gbuf.at[zs, :, pl.ds(al((1 - k) * 256, 256), 256), :], drecv.at[zs],
            ds_s.at[quarter], dr_s.at[quarter], partner,
        )

    cot_copy.wait()

    @pl.loop(0, NZ)
    def _(zz):
        term = nn(att_t[...], cot[:, pl.ds(al(zz * TOK, TOK), TOK)]).astype(BF)
        for yy in range(NY):
            gbuf[zz, yy] = term[:, 128 * yy : 128 * yy + 128]

        @pl.when(lax.rem(zz, 2) == 1)
        def _():
            pair_send(lax.div(zz, 2)).start()

        @pl.when(((zz == 0) & odd) | ((zz == 5) & even))
        def _():
            slabs_ready((3, 1))
            layer_unit(2)
            layer_unit(3)

        @pl.when((zz == 2) & even)
        def _():
            gather_first_parts()

        @pl.when((zz == 4) & odd)
        def _():
            gather_second_parts()

    layer_second(0)

    def y_first(q, side):
        return rcopy(
            gh.at[q, lax.rem(y + 2, NY), pl.ds(4 * side, 4)], yr1.at[q, side],
            y1s.at[q, side], y1r.at[q, side], at_y(1 if side == 0 else 3),
        )

    def y_second(q, side, e):
        return rcopy(
            gh.at[q, lax.rem(y + (1 if side == 0 else 3), NY), pl.ds(4 * e, 4)], yr2.at[q, side, e],
            y2s.at[q, side, e], y2r.at[q, side, e], at_y(1 if side == 0 else 3),
        )

    def early_z(d):
        return rcopy(gz.at[lax.rem(z + d, NZ)], zre.at[d - 1], zs_e.at[d], zr_e.at[d], at_z(d))

    def late_y(d):
        return rcopy(gy.at[lax.rem(y + d, NY)], yrl.at[d - 1], ys_l.at[d], yr_l.at[d], at_y(d))

    far_first = (4, 3, 5, 2, 6, 1, 7)

    def grad_pair(q):
        low, rows = CHUNKS[q]
        mine, here = pl.ds(al(k * 256 + low, 16), rows), pl.ds(low, rows)

        @pl.loop(0, NZ)
        def _(zz):
            for yy in range(NY):
                total = (gbuf[zz, yy, mine, :].astype(F32) + drecv[zz, yy, here, :].astype(F32)).astype(BF)
                if q < 2:
                    gh[q, yy, zz] = total
                else:
                    gz[zz, yy] = total

        if q < 2:
            y_first(q, 0).start()
            y_first(q, 1).start()
            y_second(q, 0, 1).start()
            y_second(q, 1, 0).start()
        else:
            for d in far_first:
                early_z(d).start()

    def grad_y_first(q):
        for side in range(2):
            y_first(q, side).wait_recv()
            owner = lax.rem(y + (1 if side == 0 else 3), NY)
            here = pl.ds(4 * side, 4)
            gh[q, owner, here] = (gh[q, owner, here].astype(F32) + yr1[q, side].astype(F32)).astype(BF)
            y_second(q, side, side).start()

    def grad_z(q, d):
        return rcopy(yh.at[q, lax.rem(z + d, NZ)], zr.at[q, d - 1], zs_g.at[q, d], zr_g.at[q, d], at_z(d))

    def grad_y_last(q):
        for side in range(2):
            for e in range(2):
                y_second(q, side, e).wait_recv()
        for e in range(2):
            here = pl.ds(4 * e, 4)
            total = gh[q, y, here].astype(F32) + yr2[q, 0, e].astype(F32) + yr2[q, 1, e].astype(F32)
            yh[q, here] = total.astype(BF)
        for d in far_first:
            grad_z(q, d).start()

    def grad_early_z():
        total = gz[z].astype(F32)
        for d in range(1, NZ):
            early_z(d).wait_recv()
            total = total + zre[d - 1].astype(F32)
        gy[...] = total.astype(BF)
        for d in (2, 1, 3):
            late_y(d).start()

    for quarter in range(4):
        pair_send(quarter).wait_recv()
    for q in range(3):
        grad_pair(q)

    @pl.when(even)
    def _():
        gather_second_parts()

    slabs_ready((1, 3))
    layer_unit(4)
    layer_unit(5)
    layer_second(1)
    gather_far_parts()
    slabs_ready((2, 2))
    layer_unit(6)
    layer_unit(7)

    @pl.loop(0, 2)
    def _(n):
        lanes = pl.ds(al(n * 256, 256), 256)
        d_o[:, lanes] = nn(cot[...], wall[:, :, :, :, lanes].reshape(4096, 256)).astype(BF)

    grad_y_first(0)

    def prepare(b, h):
        rows = pl.ds(QB * b, QB)
        heads = pl.ds(al(h * HEAD, HEAD), HEAD)
        lanes = pl.ds(al(h * QB, QB), QB)
        turned = d_o[rows, heads].astype(F32).T
        delta[b * HEADS + h] = jnp.sum(turned * att_t[heads, rows].astype(F32), axis=0, keepdims=True)
        dos[b, lanes, :] = (turned * inv_l[b * HEADS + h]).T.astype(BF)
        qs[b, lanes, :] = q_ref[rows, heads]

    def shift(b, h, low, count):
        lanes = pl.ds(al(h * QB, QB), QB)
        here = pl.ds(low - QB * b, count)
        t = b * HEADS + h
        dots = nt(vwin[pl.ds(low, count), :], d_o[pl.ds(QB * b, QB), pl.ds(al(h * HEAD, HEAD), HEAD)])
        factor = (dots - delta[t]) * (inv_l[t] * SCALE)
        dsbuf[b, here, lanes] = (pbuf[b, here, lanes].astype(F32) * factor).astype(BF)

    def key_terms(b, low, count):
        keys, here = pl.ds(low, count), pl.ds(low - QB * b, count)
        dk[keys, :] += nn(dsbuf[b, here, :], qs[b])
        dv[keys, :] += nn(pbuf[b, here, :], dos[b])

    def shift_all(b, low, count, events):
        @pl.loop(0, HEADS)
        def _(h):
            if low < 2 * TOK:
                prepare(b, h)
            shift(b, h, low, count)
            for at, event in events:

                @pl.when(h == at)
                def _():
                    event()

        key_terms(b, low, count)

    shift_all(0, 0, 1024, ((0, lambda: layer_second(2)), (1, lambda: grad_y_first(1)), (2, lambda: layer_second(3))))
    grad_y_last(0)
    shift_all(1, QB, 768, ((0, lambda: layer_second(4)), (2, lambda: layer_second(5))))

    pair_back = rcopy(gks.at[1], gkr.at[1], gs.at[1], gr.at[1], partner)
    far_back = rcopy(gks.at[0], gkr.at[0], gs.at[0], gr.at[0], at_ctx(-2))
    for s in (1, 0):
        gks[s, 0] = dk[pl.ds(s * TOK, TOK)].astype(BF)
        gks[s, 1] = dv[pl.ds(s * TOK, TOK)].astype(BF)
        if s == 1:
            pair_back.start()

    @pl.when(k == 0)
    def _():
        far_back.start()

    grad_y_last(1)
    grad_early_z()
    layer_second(6)
    shift_all(0, 1024, QB, ())
    pair_back.wait_recv()

    @pl.when(k == 1)
    def _():
        for n, acc in enumerate((dk, dv)):
            gks[0, n] = (acc[pl.ds(0, TOK)] + gkr[1, n].astype(F32)).astype(BF)
        far_back.start()

    layer_second(7)
    shift_all(1, 1024, 2 * QB, ())
    k_turned = kwin[...].astype(F32).T.astype(BF)
    for b in range(2):
        kt[b] = k_turned[:, QB * b : QB * b + KW]

    @pl.loop(0, 2 * HEADS)
    def _(t):
        b = lax.div(t, HEADS)
        h = lax.rem(t, HEADS)
        grad = nn(kt[b], dsbuf[b, :, pl.ds(al(h * QB, QB), QB)])
        qg_ref[pl.ds(al(b * QB, QB), QB), pl.ds(al(h * HEAD, HEAD), HEAD)] = grad.T.astype(BF)

    outs[1].start()

    for u in range(6):
        layer_last(u)

    sums = []
    for q in range(2):
        total = yh[q, z].astype(F32)
        for d in range(1, NZ):
            grad_z(q, d).wait_recv()
            total = total + zr[q, d - 1].astype(F32)
        sums.append(total)
    total = gy[y].astype(F32)
    for d in range(1, NY):
        late_y(d).wait_recv()
        total = total + yrl[d - 1].astype(F32)
    sums.append(total)
    turned = jnp.concatenate(sums, 0).T.astype(BF)
    fts[0] = turned[0:64]
    fts[1] = turned[64:128]

    final = rcopy(fts.at[1 - k], frec, fs, fr, partner)
    final.start()

    for u in range(6, len(UNITS)):
        layer_last(u)
    outs[0].start()

    far_back.wait_recv()
    for n, (acc, ref) in enumerate(((dk, kg_ref), (dv, vg_ref))):
        near = jnp.where(k == 0, gkr[1, n].astype(F32), 0.0)
        ref[...] = (acc[pl.ds(2 * TOK, TOK)] + gkr[0, n].astype(F32) + near).astype(BF)
        outs[2 + n].start()

    final.wait_recv()
    mine, other = fts[k], frec[...]
    pg_ref[:, 0:256] = jnp.where(k == 0, mine, other)
    pg_ref[:, 256:512] = jnp.where(k == 0, other, mine)
    outs[4].start()

    for i in range(2):
        halo_next(i).wait_send()

        @pl.when(k == 0)
        def _():
            halo_far(i).wait_send()
            halo_relay(i).wait_send()

    @pl.when(jnp.logical_not(last_y))
    def _():
        halo_next(2).wait_send()

        @pl.when(k == 0)
        def _():
            halo_far(2).wait_send()

    @pl.when(last_y)
    def _():
        values_up.wait_send()

        @pl.when(k == 0)
        def _():
            halo_next(2).wait_send()

    @pl.when(jnp.logical_not(first_y) & (k == 0))
    def _():
        halo_relay(2).wait_send()

    @pl.when(first_y)
    def _():
        values_on.wait_send()

        @pl.when(k == 1)
        def _():
            values_swap.wait_send()

    for way in range(2):
        for d in (1, 2):
            gather_z(way, d).wait_send()
            gather_on(way, d).wait_send()
        gather_relay(way).wait_send()
        for part in range(2):
            gather_y(way, part).wait_send()
    for back in range(NY):
        for part in range(2):
            pass_on(back, part).wait_send()
    for quarter in range(4):
        pair_send(quarter).wait_send()
    for q in range(2):
        for side in range(2):
            y_first(q, side).wait_send()
            for e in range(2):
                y_second(q, side, e).wait_send()
        for d in range(1, NZ):
            grad_z(q, d).wait_send()
    for d in range(1, NZ):
        early_z(d).wait_send()
    for d in range(1, NY):
        late_y(d).wait_send()
    final.wait_send()
    for u in range(len(UNITS)):
        layer_sent(u)
    pair_back.wait_send()
    far_back.wait_send()

    for copy in outs:
        copy.wait()


def finish(*refs):
    sources, targets, held, read, wrote = refs[:5], refs[5:10], refs[10:15], refs[15], refs[16]
    reads = [pltpu.make_async_copy(sources[i], held[i], read.at[i]) for i in range(5)]
    writes = [pltpu.make_async_copy(held[i], targets[i], wrote.at[i]) for i in range(5)]
    for copy in reads:
        copy.start()
    for i in range(5):
        reads[i].wait()
        writes[i].start()
    for copy in writes:
        copy.wait()


def body(doc_ids, rotated_queries, rotated_keys, value_matrix, out_proj, cotangent):
    hbm = pl.BlockSpec(memory_space=pl.ANY)
    shape = jax.ShapeDtypeStruct

    def buf(*dims, kind=BF):
        return pltpu.VMEM(dims, kind)

    out_shape = (
        shape((TOK, 1024), BF), shape((TOK, TOK), BF), shape((TOK, HEAD), BF),
        shape((TOK, HEAD), BF), shape((64, TOK), BF),
    )
    results = tuple(
        pl.pallas_call(
            kernel,
            out_shape=out_shape,
            in_specs=[hbm] * 6,
            out_specs=(hbm,) * 5,
            scratch_shapes=[
                buf(1, TOK, kind=I32), buf(TOK, TOK), buf(TOK, HEAD), buf(TOK, HEAD), buf(64, TOK),
                buf(TOK, 1024), buf(TOK, TOK), buf(TOK, HEAD), buf(TOK, HEAD), buf(64, TOK),
                buf(TOK, 4096), buf(WIN, HEAD), buf(WIN, HEAD), buf(3, 1, TOK, kind=I32),
                buf(2, HEAD, KW), buf(2, HEAD, KW), buf(NZ, NY, 2, 64, TOK), buf(2, 1, QB, kind=I32),
                buf(2, KW, HEADS * QB), buf(2, KW, HEADS * QB), buf(TOK, TOK), buf(TOK, TOK),
                buf(2 * HEADS, 1, QB, kind=F32), buf(2 * HEADS, 1, QB, kind=F32), buf(TOK, TOK),
                buf(2, HEADS * QB, HEAD), buf(2, HEADS * QB, HEAD),
                buf(WIN, HEAD, kind=F32), buf(WIN, HEAD, kind=F32),
                buf(NZ, NY, TOK, 128), buf(NZ, NY, 256, 128), buf(2, NY, NZ, 112, 128),
                buf(2, 2, 4, 112, 128), buf(2, 2, 2, 4, 112, 128), buf(2, NZ, 112, 128), buf(2, NZ - 1, 112, 128),
                buf(NZ, NY, 32, 128), buf(NZ - 1, NY, 32, 128), buf(NY, 32, 128), buf(NY - 1, 32, 128),
                buf(2, 64, 256), buf(64, 256),
                buf(8, NX, 2, QB, 128), buf(8, 2, QB, 128), buf(8, 2, 2, QB, 128),
                buf(2, 2, TOK, HEAD), buf(2, 2, TOK, HEAD),
                buf(TOK, HEAD), DMA((2,)), DMA, DMA, DMA((5,)), DMA((5,)), DMA((3, 3)), DMA((2, 3)), DMA((2, 2)), DMA((2, 2)), DMA((2, 2)), DMA((2, 2)),
                DMA((2, 2)), DMA((2, 2)), DMA((2,)), DMA((2,)), DMA((NY, 2)), DMA((NY, 2)),
                DMA((4,)), DMA((4,)), DMA((2, 2)), DMA((2, 2)), DMA((2, 2, 2)), DMA((2, 2, 2)),
                DMA((2, NZ)), DMA((2, NZ)), DMA((NZ,)), DMA((NZ,)), DMA((NY,)), DMA((NY,)), DMA, DMA,
                DMA((8, 2)), DMA((8, 2)), DMA((8, 2, 2)), DMA((8, 2, 2)), DMA((2,)), DMA((2,)),
            ],
            compiler_params=pltpu.CompilerParams(
                collective_id=0, has_side_effects=True, vmem_limit_bytes=VMEM_LIMIT
            ),
        )(doc_ids.reshape(1, TOK), rotated_queries, rotated_keys, value_matrix, out_proj, cotangent)
    )
    return tuple(
        pl.pallas_call(
            finish,
            out_shape=out_shape,
            in_specs=[hbm] * 5,
            out_specs=(hbm,) * 5,
            scratch_shapes=[pltpu.VMEM(o.shape, o.dtype) for o in out_shape] + [DMA((5,)), DMA((5,))],
            compiler_params=pltpu.CompilerParams(vmem_limit_bytes=VMEM_LIMIT),
        )(*results)
    )


def solution(mesh):
    in_specs = (P("ctx"), P("ctx", "hg"), P("ctx", "hg"), P("ctx", "hg"), P("ctx", "hg"), P("ctx", None))
    out_specs = (P("ctx", "hg"),) * 5
    return jax.shard_map(body, mesh=mesh, in_specs=in_specs, out_specs=out_specs, check_vma=False)
```

```python
import jax
import jax.numpy as jnp
from jax import lax
from jax.experimental import pallas as pl
from jax.experimental.pallas import tpu as pltpu
from jax.sharding import PartitionSpec as P

MESH = pl.DeviceIdType.MESH
BF = jnp.bfloat16
F32 = jnp.float32
I32 = jnp.int32
DMA = pltpu.SemaphoreType.DMA

HEAD = 128
HEADS = 4
TOK = 512
QB = 256
KW = 1280
WIN = 1536
NX, NY, NZ = 4, 4, 8
CTX = 64
SCALE = HEAD ** (-0.5)
EXP_SCALE = SCALE * 1.4426950408889634
MASKED = -1e30
VMEM_LIMIT = 64 * 1024 * 1024 - 65536
UNITS = (
    (0, (0, 0)), (1, (0, 0)), (0, (3, 1)), (1, (3, 1)), (0, (1, 3)), (1, (1, 3)), (0, (2, 2)), (1, (2, 2)),
)
CHUNKS = ((0, 96), (96, 96), (192, 64))


def nn(a, b):
    return jnp.dot(a, b, preferred_element_type=F32)


def nt(a, b):
    return lax.dot_general(a, b, (((1,), (1,)), ((), ())), preferred_element_type=F32)


def al(value, by):
    return pl.multiple_of(value, by)


def kernel(
    doc_hbm, q_hbm, k_hbm, v_hbm, w_hbm, cot_hbm,
    out_hbm, qg_hbm, kg_hbm, vg_hbm, pg_hbm,
    doc_ref, q_ref, k_ref, v_ref, w_ref, out_ref, qg_ref, kg_ref, vg_ref, pg_ref,
    cot, kwin, vwin, dwin, kt, vt, wall, st_ref, pbuf, dsbuf, att_t, att, inv_l, delta, d_o, dos, qs, dk, dv,
    gbuf, drecv, gh, yr1, yr2, yh, zr, gz, zre, gy, yrl, fts, frec, lbuf, xr1, xr2, gks, gkr,
    vrel, vs, vr, cot_sem, in_sem, out_sem, hs, hr, az_s, az_r, ao_s, ao_r, ys_w, yr_w, rs_w, rr_w, ps_w, pr_w,
    ds_s, dr_s, y1s, y1r, y2s, y2r, zs_g, zr_g, zs_e, zr_e, ys_l, yr_l, fs, fr, x1s, x1r, x2s, x2r, gs, gr,
):
    c = lax.axis_index("ctx")
    x = lax.axis_index("hg")
    z = lax.div(c, 8)
    y = lax.rem(lax.div(c, 2), NY)
    k = lax.rem(c, 2)

    def at_ctx(by):
        return (lax.rem(c + by + CTX, CTX), x)

    def at_z(by):
        return (lax.rem(z + by, NZ) * 8 + y * 2 + k, x)

    def at_y(by):
        return (z * 8 + lax.rem(y + by, NY) * 2 + k, x)

    def at_x(by):
        return (c, lax.rem(x + by, NX))

    partner = (z * 8 + y * 2 + (1 - k), x)

    def rcopy(src, dst, send, recv, device):
        return pltpu.make_async_remote_copy(
            src_ref=src, dst_ref=dst, send_sem=send, recv_sem=recv,
            device_id=device, device_id_type=MESH,
        )

    barrier = pltpu.get_barrier_semaphore()
    peers = [partner, at_y(1), at_y(3), at_x(1), at_x(3), at_ctx(1), at_ctx(2), at_ctx(-1), at_ctx(-2)]
    peers += [at_z(d) for d in range(1, NZ)]
    for peer in peers:
        pl.semaphore_signal(barrier, inc=1, device_id=peer, device_id_type=MESH)
    ins = ((w_hbm, w_ref), (k_hbm, k_ref), (doc_hbm, doc_ref), (v_hbm, v_ref), (q_hbm, q_ref))
    ins = [pltpu.make_async_copy(src, dst, in_sem.at[i]) for i, (src, dst) in enumerate(ins)]
    outs = ((out_ref, out_hbm), (qg_ref, qg_hbm), (kg_ref, kg_hbm), (vg_ref, vg_hbm), (pg_ref, pg_hbm))
    outs = [pltpu.make_async_copy(src, dst, out_sem.at[i]) for i, (src, dst) in enumerate(outs)]
    cot_copy = pltpu.make_async_copy(cot_hbm, cot, cot_sem)
    for copy in ins:
        copy.start()
    cot_copy.start()
    for copy in ins:
        copy.wait()
    pl.semaphore_wait(barrier, len(peers))

    own_parts = ((doc_ref, dwin, 0), (k_ref, kwin, 1), (v_ref, vwin, 2))

    def piece(ref, index, at):
        return ref.at[at] if index == 0 else ref.at[pl.ds(at * TOK, TOK)]

    def halo_next(i):
        mine, ref, n = own_parts[i]
        return rcopy(mine, piece(ref, n, 1), hs.at[0, n], hr.at[1, n], at_ctx(1))

    def halo_far(i):
        mine, ref, n = own_parts[i]
        return rcopy(mine, piece(ref, n, 0), hs.at[1, n], hr.at[0, n], at_ctx(2))

    def halo_relay(i):
        _, ref, n = own_parts[i]
        return rcopy(piece(ref, n, 1), piece(ref, n, 0), hs.at[2, n], hr.at[0, n], partner)

    def shard(zz):
        return wall.at[zz, y, k]

    def gather_z(way, d):
        to = at_z(d if way == 0 else NZ - d)
        return rcopy(w_ref, shard(z), az_s.at[way, d - 1], az_r.at[way, d - 1], to)

    def gather_on(way, d):
        zz = lax.rem(z + (NZ - 2 if way == 0 else 2), NZ)
        rows = pl.ds(0, 64) if d == 1 else pl.ds(32 * way, 32)
        src = wall.at[zz, y, k, rows]
        return rcopy(src, src, ao_s.at[way, d - 1], ao_r.at[way, d - 1], at_z(d if way == 0 else NZ - d))

    def slab(back, part):
        return wall.at[pl.ds(4 * part, 4), lax.rem(y + back, NY), k]

    def gather_y(side, part):
        return rcopy(slab(0, part), slab(0, part), ys_w.at[side, part], yr_w.at[side, part], at_y(1 if side == 0 else 3))

    def gather_relay(side):
        src = slab(3 if side == 0 else 1, side)
        return rcopy(src, src, rs_w.at[side], rr_w.at[side], at_y(1 if side == 0 else 3))

    def pass_on(back, part):
        return rcopy(slab(back, part), slab(back, part), ps_w.at[back, part], pr_w.at[back, part], partner)

    def gather_first_parts():
        for side in range(2):
            gather_y(side, side).wait_recv()
            gather_relay(side).start()
            pass_on(3 if side == 0 else 1, side).start()

    def gather_second_parts():
        for side in range(2):
            gather_y(side, 1 - side).wait_recv()
            pass_on(3 if side == 0 else 1, 1 - side).start()

    def gather_far_parts():
        for side in range(2):
            gather_relay(side).wait_recv()
            pass_on(2, side).start()

    def slabs_ready(backs):
        for part in range(2):
            pass_on(backs[part], part).wait_recv()

    def halo_starts(i):
        halo_next(i).start()

        @pl.when(k == 0)
        def _():
            halo_far(i).start()

    last_y = y == NY - 1
    first_y = y == 0
    values_up = rcopy(v_ref, vrel, vs.at[0], vr, at_y(1))
    values_on = rcopy(vrel, piece(vwin, 2, 0), vs.at[1], hr.at[0, 2], at_z(1))
    values_swap = rcopy(piece(vwin, 2, 0), piece(vwin, 2, 1), hs.at[2, 2], hr.at[1, 2], partner)

    halo_starts(0)
    halo_starts(1)

    @pl.when(jnp.logical_not(last_y))
    def _():
        halo_starts(2)

    @pl.when(last_y)
    def _():
        values_up.start()

        @pl.when(k == 0)
        def _():
            halo_next(2).start()

    for d in (2, 1):
        for way in range(2):
            gather_z(way, d).start()

    wall[z, y, k] = w_ref[...]
    kwin[pl.ds(2 * TOK, TOK)] = k_ref[...]
    vwin[pl.ds(2 * TOK, TOK)] = v_ref[...]
    dwin[2] = doc_ref[...]
    dk[...] = jnp.zeros_like(dk)
    dv[...] = jnp.zeros_like(dv)

    def gather_middle():
        for way in range(2):
            gather_z(way, 2).wait_recv()
            gather_on(way, 2).start()
            gather_on(way, 1).start()

    def halo_arrives(i):
        halo_next(i).wait_recv()

        @pl.when(k == 0)
        def _():
            halo_relay(i).start()

    def gather_along_y():
        for way in range(2):
            gather_z(way, 1).wait_recv()
            gather_on(way, 1).wait_recv()
        for way in range(2):
            gather_on(way, 2).wait_recv()
        for part in range(2):
            for side in range(2):
                gather_y(side, part if side == 0 else 1 - part).start()
        for part in range(2):
            pass_on(0, part).start()

    halo_arrives(0)
    halo_arrives(1)

    @pl.when(jnp.logical_not(last_y))
    def _():
        gather_middle()

    for i in range(2):
        halo_far(i).wait_recv()

    doc_row = dwin[2].astype(F32)
    start = jnp.zeros((1, TOK), F32)
    for p in range(3):
        column = jnp.broadcast_to(dwin[p].astype(F32), (128, TOK)).T
        counts = [
            jnp.sum(jnp.where(column < doc_row[:, 128 * b : 128 * b + 128], 1.0, 0.0), axis=0, keepdims=True)
            for b in range(TOK // 128)
        ]
        count = jnp.concatenate(counts, 1)
        start = start + (jnp.where(c >= 2 - p, count, float(TOK)) if p < 2 else count)
    start = start.astype(I32)
    for b in range(2):
        st_ref[b] = start[:, QB * b : QB * b + QB] - QB * b

    def x_first(u, side):
        return rcopy(lbuf.at[u, 2, side], xr1.at[u, side], x1s.at[u, side], x1r.at[u, side], at_x(1 if side == 0 else 3))

    def x_second(u, side, e):
        return rcopy(
            lbuf.at[u, 1 if side == 0 else 3, e], xr2.at[u, side, e], x2s.at[u, side, e], x2r.at[u, side, e],
            at_x(1 if side == 0 else 3),
        )

    def layer_unit(u):
        b, backs = UNITS[u]
        for part in range(2):
            rows = wall[pl.ds(4 * part, 4), lax.rem(y + backs[part], NY)].reshape(TOK, TOK)
            term = nt(att[pl.ds(b * QB, QB)], rows).astype(BF)
            for owner in range(2):
                for e in range(2):
                    at = 256 * owner + 128 * e
                    lbuf[u, lax.rem(2 * part + owner - x + NX, NX), e] = term[:, at : at + 128]
        x_first(u, 0).start()
        x_first(u, 1).start()
        x_second(u, 0, 1).start()
        x_second(u, 1, 0).start()

    def layer_second(u):
        for side in range(2):
            x_first(u, side).wait_recv()
            r = 1 if side == 0 else 3
            lbuf[u, r, side] = (lbuf[u, r, side].astype(F32) + xr1[u, side].astype(F32)).astype(BF)
            x_second(u, side, side).start()

    def layer_last(u):
        b, backs = UNITS[u]
        back = jnp.where(x < 2, backs[0], backs[1])
        for e in range(2):
            for side in range(2):
                x_second(u, side, e).wait_recv()
            total = lbuf[u, 0, e].astype(F32) + xr2[u, 0, e].astype(F32) + xr2[u, 1, e].astype(F32)
            lanes = pl.ds(al(512 * e + 128 * lax.rem(y + back, NY), 128), 128)
            out_ref[pl.ds(b * QB, QB), lanes] = total.astype(BF)

    def layer_sent(u):
        for side in range(2):
            x_first(u, side).wait_send()
            for e in range(2):
                x_second(u, side, e).wait_send()

    def attend(t):
        b = lax.div(t, HEADS)
        h = lax.rem(t, HEADS)
        rows = pl.ds(al(b * QB, QB), QB)
        heads = pl.ds(al(h * HEAD, HEAD), HEAD)
        scores = nt(kwin[pl.ds(al(b * QB, QB), KW), :], q_ref[rows, heads])
        key_at = lax.broadcasted_iota(I32, (KW, QB), 0)
        last = lax.broadcasted_iota(I32, (1, QB), 1) + 2 * TOK
        scores = jnp.where((key_at >= st_ref[b]) & (key_at <= last), scores, MASKED)
        top = jnp.max(scores, axis=0, keepdims=True)
        weights = jnp.exp2(scores * EXP_SCALE - top * EXP_SCALE)
        inv_l[t] = 1.0 / jnp.sum(weights, axis=0, keepdims=True)
        pbuf[b, :, pl.ds(al(h * QB, QB), QB)] = weights.astype(BF)

    def gather_values(t):
        b = lax.div(t, HEADS)
        h = lax.rem(t, HEADS)
        rows = pl.ds(al(b * QB, QB), QB)
        heads = pl.ds(al(h * HEAD, HEAD), HEAD)
        turned = nn(vt[b], pbuf[b, :, pl.ds(al(h * QB, QB), QB)]) * inv_l[t]
        att_t[heads, rows] = turned.astype(BF)
        att[rows, heads] = turned.T.astype(BF)

    @pl.loop(0, HEADS)
    def _(t):
        attend(t)

        @pl.when((t == 0) & first_y)
        def _():
            values_up.wait_recv()
            values_on.start()

        @pl.when((t == 1) & last_y)
        def _():
            gather_middle()

        @pl.when((t == 1) & jnp.logical_not(last_y))
        def _():
            gather_along_y()

    @pl.when(first_y)
    def _():
        halo_far(2).wait_recv()

        @pl.when(k == 1)
        def _():
            values_swap.start()

        halo_next(2).wait_recv()

    @pl.when(jnp.logical_not(first_y))
    def _():
        halo_arrives(2)
        halo_far(2).wait_recv()

    v_turned = vwin[...].astype(F32).T.astype(BF)
    for b in range(2):
        vt[b] = v_turned[:, QB * b : QB * b + KW]

    odd = lax.rem(y, 2) == 1
    even = jnp.logical_not(odd)

    @pl.loop(0, HEADS)
    def _(t):
        gather_values(t)

        @pl.when((t == 0) & last_y)
        def _():
            gather_along_y()

    slabs_ready((0, 0))
    layer_unit(0)

    @pl.loop(HEADS, 2 * HEADS)
    def _(t):
        attend(t)
        gather_values(t)

        @pl.when((t == 6) & odd)
        def _():
            gather_first_parts()

    layer_unit(1)

    def pair_send(quarter):
        zs = pl.ds(al(2 * quarter, 2), 2)
        return rcopy(
            gbuf.at[zs, :, pl.ds(al((1 - k) * 256, 256), 256), :], drecv.at[zs],
            ds_s.at[quarter], dr_s.at[quarter], partner,
        )

    cot_copy.wait()

    @pl.loop(0, NZ)
    def _(zz):
        term = nn(att_t[...], cot[:, pl.ds(al(zz * TOK, TOK), TOK)]).astype(BF)
        for yy in range(NY):
            gbuf[zz, yy] = term[:, 128 * yy : 128 * yy + 128]

        @pl.when(lax.rem(zz, 2) == 1)
        def _():
            pair_send(lax.div(zz, 2)).start()

        @pl.when(((zz == 0) & odd) | ((zz == 5) & even))
        def _():
            slabs_ready((3, 1))
            layer_unit(2)
            layer_unit(3)

        @pl.when((zz == 2) & even)
        def _():
            gather_first_parts()

        @pl.when((zz == 4) & odd)
        def _():
            gather_second_parts()

    layer_second(0)

    def y_first(q, side):
        return rcopy(
            gh.at[q, lax.rem(y + 2, NY), pl.ds(4 * side, 4)], yr1.at[q, side],
            y1s.at[q, side], y1r.at[q, side], at_y(1 if side == 0 else 3),
        )

    def y_second(q, side, e):
        return rcopy(
            gh.at[q, lax.rem(y + (1 if side == 0 else 3), NY), pl.ds(4 * e, 4)], yr2.at[q, side, e],
            y2s.at[q, side, e], y2r.at[q, side, e], at_y(1 if side == 0 else 3),
        )

    def early_z(d):
        return rcopy(gz.at[lax.rem(z + d, NZ)], zre.at[d - 1], zs_e.at[d], zr_e.at[d], at_z(d))

    def late_y(d):
        return rcopy(gy.at[lax.rem(y + d, NY)], yrl.at[d - 1], ys_l.at[d], yr_l.at[d], at_y(d))

    far_first = (4, 3, 5, 2, 6, 1, 7)

    def grad_pair(q):
        low, rows = CHUNKS[q]
        mine, here = pl.ds(al(k * 256 + low, 32), rows), pl.ds(low, rows)

        @pl.loop(0, NZ)
        def _(zz):
            for yy in range(NY):
                total = (gbuf[zz, yy, mine, :].astype(F32) + drecv[zz, yy, here, :].astype(F32)).astype(BF)
                if q < 2:
                    gh[q, yy, zz] = total
                else:
                    gz[zz, yy] = total

        if q < 2:
            y_first(q, 0).start()
            y_first(q, 1).start()
            y_second(q, 0, 1).start()
            y_second(q, 1, 0).start()
        else:
            for d in far_first:
                early_z(d).start()

    def grad_y_first(q):
        for side in range(2):
            y_first(q, side).wait_recv()
            owner = lax.rem(y + (1 if side == 0 else 3), NY)
            here = pl.ds(4 * side, 4)
            gh[q, owner, here] = (gh[q, owner, here].astype(F32) + yr1[q, side].astype(F32)).astype(BF)
            y_second(q, side, side).start()

    def grad_z(q, d):
        return rcopy(yh.at[q, lax.rem(z + d, NZ)], zr.at[q, d - 1], zs_g.at[q, d], zr_g.at[q, d], at_z(d))

    def grad_y_last(q):
        for side in range(2):
            for e in range(2):
                y_second(q, side, e).wait_recv()
        for e in range(2):
            here = pl.ds(4 * e, 4)
            total = gh[q, y, here].astype(F32) + yr2[q, 0, e].astype(F32) + yr2[q, 1, e].astype(F32)
            yh[q, here] = total.astype(BF)
        for d in far_first:
            grad_z(q, d).start()

    def grad_early_z():
        total = gz[z].astype(F32)
        for d in range(1, NZ):
            early_z(d).wait_recv()
            total = total + zre[d - 1].astype(F32)
        gy[...] = total.astype(BF)
        for d in (2, 1, 3):
            late_y(d).start()

    for quarter in range(4):
        pair_send(quarter).wait_recv()
    for q in range(3):
        grad_pair(q)

    @pl.when(even)
    def _():
        gather_second_parts()

    slabs_ready((1, 3))
    layer_unit(4)
    layer_unit(5)
    layer_second(1)
    gather_far_parts()
    slabs_ready((2, 2))
    layer_unit(6)
    layer_unit(7)

    @pl.loop(0, 2)
    def _(n):
        lanes = pl.ds(al(n * 256, 256), 256)
        d_o[:, lanes] = nn(cot[...], wall[:, :, :, :, lanes].reshape(4096, 256)).astype(BF)

    grad_y_first(0)

    def prepare(b, h):
        rows = pl.ds(QB * b, QB)
        heads = pl.ds(al(h * HEAD, HEAD), HEAD)
        lanes = pl.ds(al(h * QB, QB), QB)
        turned = d_o[rows, heads].astype(F32).T
        delta[b * HEADS + h] = jnp.sum(turned * att_t[heads, rows].astype(F32), axis=0, keepdims=True)
        dos[b, lanes, :] = (turned * inv_l[b * HEADS + h]).T.astype(BF)
        qs[b, lanes, :] = q_ref[rows, heads]

    def shift(b, h, low, count):
        lanes = pl.ds(al(h * QB, QB), QB)
        here = pl.ds(low - QB * b, count)
        t = b * HEADS + h
        dots = nt(vwin[pl.ds(low, count), :], d_o[pl.ds(QB * b, QB), pl.ds(al(h * HEAD, HEAD), HEAD)])
        factor = (dots - delta[t]) * (inv_l[t] * SCALE)
        dsbuf[b, here, lanes] = (pbuf[b, here, lanes].astype(F32) * factor).astype(BF)

    def key_terms(b, low, count):
        keys, here = pl.ds(low, count), pl.ds(low - QB * b, count)
        dk[keys, :] += nn(dsbuf[b, here, :], qs[b])
        dv[keys, :] += nn(pbuf[b, here, :], dos[b])

    def shift_all(b, low, count, events):
        @pl.loop(0, HEADS)
        def _(h):
            if low < 2 * TOK:
                prepare(b, h)
            shift(b, h, low, count)
            for at, event in events:

                @pl.when(h == at)
                def _():
                    event()

        key_terms(b, low, count)

    shift_all(0, 0, 1024, ((0, lambda: layer_second(2)), (1, lambda: grad_y_first(1)), (2, lambda: layer_second(3))))
    grad_y_last(0)
    shift_all(1, QB, 768, ((0, lambda: layer_second(4)), (2, lambda: layer_second(5)), (3, lambda: grad_y_last(1))))

    pair_back = rcopy(gks.at[1], gkr.at[1], gs.at[1], gr.at[1], partner)
    far_back = rcopy(gks.at[0], gkr.at[0], gs.at[0], gr.at[0], at_ctx(-2))
    for s in (1, 0):
        gks[s, 0] = dk[pl.ds(s * TOK, TOK)].astype(BF)
        gks[s, 1] = dv[pl.ds(s * TOK, TOK)].astype(BF)
        if s == 1:
            pair_back.start()

    @pl.when(k == 0)
    def _():
        far_back.start()

    grad_early_z()
    layer_second(6)
    shift_all(0, 1024, QB, ())
    pair_back.wait_recv()

    @pl.when(k == 1)
    def _():
        for n, acc in enumerate((dk, dv)):
            gks[0, n] = (acc[pl.ds(0, TOK)] + gkr[1, n].astype(F32)).astype(BF)
        far_back.start()

    layer_second(7)
    shift_all(1, 1024, 2 * QB, ())
    k_turned = kwin[...].astype(F32).T.astype(BF)
    for b in range(2):
        kt[b] = k_turned[:, QB * b : QB * b + KW]

    @pl.loop(0, 2 * HEADS)
    def _(t):
        b = lax.div(t, HEADS)
        h = lax.rem(t, HEADS)
        grad = nn(kt[b], dsbuf[b, :, pl.ds(al(h * QB, QB), QB)])
        qg_ref[pl.ds(al(b * QB, QB), QB), pl.ds(al(h * HEAD, HEAD), HEAD)] = grad.T.astype(BF)

    outs[1].start()

    for u in range(6):
        layer_last(u)

    sums = []
    for q in range(2):
        total = yh[q, z].astype(F32)
        for d in range(1, NZ):
            grad_z(q, d).wait_recv()
            total = total + zr[q, d - 1].astype(F32)
        sums.append(total)
    total = gy[y].astype(F32)
    for d in range(1, NY):
        late_y(d).wait_recv()
        total = total + yrl[d - 1].astype(F32)
    sums.append(total)
    turned = jnp.concatenate(sums, 0).T.astype(BF)
    fts[0] = turned[0:64]
    fts[1] = turned[64:128]

    final = rcopy(fts.at[1 - k], frec, fs, fr, partner)
    final.start()

    for u in range(6, len(UNITS)):
        layer_last(u)
    outs[0].start()

    far_back.wait_recv()
    for n, (acc, ref) in enumerate(((dk, kg_ref), (dv, vg_ref))):
        near = jnp.where(k == 0, gkr[1, n].astype(F32), 0.0)
        ref[...] = (acc[pl.ds(2 * TOK, TOK)] + gkr[0, n].astype(F32) + near).astype(BF)
        outs[2 + n].start()

    final.wait_recv()
    mine, other = fts[k], frec[...]
    pg_ref[:, 0:256] = jnp.where(k == 0, mine, other)
    pg_ref[:, 256:512] = jnp.where(k == 0, other, mine)
    outs[4].start()

    for i in range(2):
        halo_next(i).wait_send()

        @pl.when(k == 0)
        def _():
            halo_far(i).wait_send()
            halo_relay(i).wait_send()

    @pl.when(jnp.logical_not(last_y))
    def _():
        halo_next(2).wait_send()

        @pl.when(k == 0)
        def _():
            halo_far(2).wait_send()

    @pl.when(last_y)
    def _():
        values_up.wait_send()

        @pl.when(k == 0)
        def _():
            halo_next(2).wait_send()

    @pl.when(jnp.logical_not(first_y) & (k == 0))
    def _():
        halo_relay(2).wait_send()

    @pl.when(first_y)
    def _():
        values_on.wait_send()

        @pl.when(k == 1)
        def _():
            values_swap.wait_send()

    for way in range(2):
        for d in (1, 2):
            gather_z(way, d).wait_send()
            gather_on(way, d).wait_send()
        gather_relay(way).wait_send()
        for part in range(2):
            gather_y(way, part).wait_send()
    for back in range(NY):
        for part in range(2):
            pass_on(back, part).wait_send()
    for quarter in range(4):
        pair_send(quarter).wait_send()
    for q in range(2):
        for side in range(2):
            y_first(q, side).wait_send()
            for e in range(2):
                y_second(q, side, e).wait_send()
        for d in range(1, NZ):
            grad_z(q, d).wait_send()
    for d in range(1, NZ):
        early_z(d).wait_send()
    for d in range(1, NY):
        late_y(d).wait_send()
    final.wait_send()
    for u in range(len(UNITS)):
        layer_sent(u)
    pair_back.wait_send()
    far_back.wait_send()

    for copy in outs:
        copy.wait()


def finish(*refs):
    sources, targets, held, read, wrote = refs[:5], refs[5:10], refs[10:15], refs[15], refs[16]
    reads = [pltpu.make_async_copy(sources[i], held[i], read.at[i]) for i in range(5)]
    writes = [pltpu.make_async_copy(held[i], targets[i], wrote.at[i]) for i in range(5)]
    for copy in reads:
        copy.start()
    for i in range(5):
        reads[i].wait()
        writes[i].start()
    for copy in writes:
        copy.wait()


def body(doc_ids, rotated_queries, rotated_keys, value_matrix, out_proj, cotangent):
    hbm = pl.BlockSpec(memory_space=pl.ANY)
    shape = jax.ShapeDtypeStruct

    def buf(*dims, kind=BF):
        return pltpu.VMEM(dims, kind)

    out_shape = (
        shape((TOK, 1024), BF), shape((TOK, TOK), BF), shape((TOK, HEAD), BF),
        shape((TOK, HEAD), BF), shape((64, TOK), BF),
    )
    results = tuple(
        pl.pallas_call(
            kernel,
            out_shape=out_shape,
            in_specs=[hbm] * 6,
            out_specs=(hbm,) * 5,
            scratch_shapes=[
                buf(1, TOK, kind=I32), buf(TOK, TOK), buf(TOK, HEAD), buf(TOK, HEAD), buf(64, TOK),
                buf(TOK, 1024), buf(TOK, TOK), buf(TOK, HEAD), buf(TOK, HEAD), buf(64, TOK),
                buf(TOK, 4096), buf(WIN, HEAD), buf(WIN, HEAD), buf(3, 1, TOK, kind=I32),
                buf(2, HEAD, KW), buf(2, HEAD, KW), buf(NZ, NY, 2, 64, TOK), buf(2, 1, QB, kind=I32),
                buf(2, KW, HEADS * QB), buf(2, KW, HEADS * QB), buf(TOK, TOK), buf(TOK, TOK),
                buf(2 * HEADS, 1, QB, kind=F32), buf(2 * HEADS, 1, QB, kind=F32), buf(TOK, TOK),
                buf(2, HEADS * QB, HEAD), buf(2, HEADS * QB, HEAD),
                buf(WIN, HEAD, kind=F32), buf(WIN, HEAD, kind=F32),
                buf(NZ, NY, TOK, 128), buf(NZ, NY, 256, 128), buf(2, NY, NZ, 96, 128),
                buf(2, 2, 4, 96, 128), buf(2, 2, 2, 4, 96, 128), buf(2, NZ, 96, 128), buf(2, NZ - 1, 96, 128),
                buf(NZ, NY, 64, 128), buf(NZ - 1, NY, 64, 128), buf(NY, 64, 128), buf(NY - 1, 64, 128),
                buf(2, 64, 256), buf(64, 256),
                buf(8, NX, 2, QB, 128), buf(8, 2, QB, 128), buf(8, 2, 2, QB, 128),
                buf(2, 2, TOK, HEAD), buf(2, 2, TOK, HEAD),
                buf(TOK, HEAD), DMA((2,)), DMA, DMA, DMA((5,)), DMA((5,)), DMA((3, 3)), DMA((2, 3)), DMA((2, 2)), DMA((2, 2)), DMA((2, 2)), DMA((2, 2)),
                DMA((2, 2)), DMA((2, 2)), DMA((2,)), DMA((2,)), DMA((NY, 2)), DMA((NY, 2)),
                DMA((4,)), DMA((4,)), DMA((2, 2)), DMA((2, 2)), DMA((2, 2, 2)), DMA((2, 2, 2)),
                DMA((2, NZ)), DMA((2, NZ)), DMA((NZ,)), DMA((NZ,)), DMA((NY,)), DMA((NY,)), DMA, DMA,
                DMA((8, 2)), DMA((8, 2)), DMA((8, 2, 2)), DMA((8, 2, 2)), DMA((2,)), DMA((2,)),
            ],
            compiler_params=pltpu.CompilerParams(
                collective_id=0, has_side_effects=True, vmem_limit_bytes=VMEM_LIMIT
            ),
        )(doc_ids.reshape(1, TOK), rotated_queries, rotated_keys, value_matrix, out_proj, cotangent)
    )
    return tuple(
        pl.pallas_call(
            finish,
            out_shape=out_shape,
            in_specs=[hbm] * 5,
            out_specs=(hbm,) * 5,
            scratch_shapes=[pltpu.VMEM(o.shape, o.dtype) for o in out_shape] + [DMA((5,)), DMA((5,))],
            compiler_params=pltpu.CompilerParams(vmem_limit_bytes=VMEM_LIMIT),
        )(*results)
    )


def solution(mesh):
    in_specs = (P("ctx"), P("ctx", "hg"), P("ctx", "hg"), P("ctx", "hg"), P("ctx", "hg"), P("ctx", None))
    out_specs = (P("ctx", "hg"),) * 5
    return jax.shard_map(body, mesh=mesh, in_specs=in_specs, out_specs=out_specs, check_vma=False)
```
